768 devices in a mesh: dp: 12 (over z_lo, core), enc: 64 (over z_hi, y, x).
Axes of the slice: x: 4, y: 8, z: 12 (z_hi: 2, z_lo: 6; z = z_hi * 6 + z_lo), core: 2. Of those that a mesh axis runs over, the one named last changes fastest.
Arguments:
- counts: int32 [12, 64], P('dp'), may hold values from 1 to 48, 1536 in all within a row
- pixels: bfloat16 [12, 49152, 392], P('dp', 'enc'), may hold values from -6 to 6
- cotangent: bfloat16 [12, 24576, 1728], P('dp', 'enc'), may hold values from -0.03125 to 0.03125
Outputs:
- grad_patch: float32 [1728, 392], P('enc')
The draws below stay inside these ranges and needn't reach their ends.
Inputs may be any that keep to these rules, and one draw needn't show every extreme that they name: `counts`: each row of a group sums to exactly 1536; in each row some device holds exactly 48 live blocks.
All inputs are finite; a program needn't handle non-finite values.
Results may differ from the reference program's by a relative error of at most 0.0003.
Values may be sent and summed in bfloat16 or wider, within the bound.
No kernel may reach another device: no remote copies, remote signals or barrier semaphores. Data moves between devices by JAX's collectives and lax.ppermute only.
A program may use at most 32 MiB of HBM per device.

```python
import math
import jax
import jax.numpy as jnp
import numpy as np
from jax import lax

D = 1728
PIX = 392
BLK = 16
OWNED = 24
IN_ROWS = 49152
OWN_ROWS = 24576
N_DP = 12
N_ENC = 64


def raised(values, key, source, target, blocks, factor):
    def block_of(axis_at):
        return (jnp.arange(values.shape[axis_at]) // (values.shape[axis_at] // blocks)).reshape((-1,) + (1,) * (values.ndim - 1 - axis_at))

    one_side = jax.random.permutation(key, blocks)[block_of(target)]
    far = (block_of(target) + blocks // 2) % blocks
    return jnp.where((block_of(source) == one_side) | (block_of(source) == far), factor * values, values)


def steps_of(key, extent, cuts, low, high):
    gain, own = 1.0, jax.random.fold_in(key, 6)
    for position, shards_of in cuts:
        draws = jnp.exp(jax.random.uniform(jax.random.fold_in(own, position), (shards_of,), jnp.float32, low / len(cuts), high / len(cuts)))
        gain = gain * jnp.repeat(draws, extent[position] // shards_of).reshape([-1 if axis == position else 1 for axis in range(len(extent))])
    return gain


def split_up(count, total, most, skew):
    loads = [(1 << 20) // math.isqrt(rank ** skew) + 1 for rank in range(2, count + 1)]
    rest, holding = total - most - (count - 1), [1] * (count - 1)
    while rest > 0:
        candidates = [i for i in range(count - 1) if holding[i] < most]
        mass, left = sum([loads[i] for i in candidates]), rest
        for i in candidates:
            more = min(most - holding[i], max(1, left * loads[i] // mass), rest)
            holding[i] = holding[i] + more
            rest = rest - more
    return np.array([most] + holding)


def uneven(rng, number_of, total, most, skew):
    if number_of == 2:
        one = jax.random.randint(rng, (), max(1, total - most), min(most, total - 1) + 1)
        return jnp.stack([one, total - one])
    lengths = jnp.asarray(split_up(number_of, total, most, skew), jnp.int32)
    pairs = (number_of - 1) // 2
    giver, sink = lengths[1:1 + 2 * pairs:2], lengths[2:2 + 2 * pairs:2]
    room = jnp.minimum(giver - 1, most - sink)
    passed = jax.random.randint(jax.random.fold_in(rng, 1), (pairs,), 0, 1 << 20) % (room + 1)
    lengths = lengths.at[1:1 + 2 * pairs:2].set(giver - passed).at[2:2 + 2 * pairs:2].set(sink + passed)
    return lengths[jax.random.permutation(jax.random.fold_in(rng, 2), number_of)]


def normal_values(own_key, dims, spread, reach, split=(), held_as=jnp.bfloat16):
    array = jax.random.normal(own_key, dims, jnp.float32) * spread
    if len(split) > 0:
        array = steps_of(own_key, dims, split, -0.22, 0.18) * array
    return jnp.clip(array, min=-reach, max=reach).astype(held_as)


def gaussian_with(own_key, extent, width, most, cuts, heavy, kind=jnp.bfloat16):
    array = width * jax.random.normal(own_key, extent, jnp.float32)
    if cuts:
        array = array * steps_of(own_key, extent, cuts, -0.22, 0.18)
    return jnp.clip(raised(array, jax.random.fold_in(own_key, 3), *heavy), -most, most).astype(kind)


def setup_inputs(seed: int = 0) -> dict:
    key_of = jax.random.split(jax.random.key(seed), 4)
    counts = jax.vmap(lambda own: uneven(own, N_ENC, OWNED * N_ENC, 2 * OWNED, 2))(jax.random.split(key_of[0], N_DP)).reshape((N_DP, N_ENC)).astype(jnp.int32)
    pixels = normal_values(key_of[1], (N_DP, IN_ROWS, PIX), 1.0, 6.0, ((0, 12), (1, 64)))
    cotangent = gaussian_with(key_of[2], (N_DP, OWN_ROWS, D), (N_DP * N_ENC * OWNED * BLK) ** -0.5, 0.03125, ((0, 12), (1, 64)), (1, 2, 64, 4.0))
    return dict(counts=counts, pixels=pixels, cotangent=cotangent)


def reference(counts, pixels, cotangent):
    n_enc = counts.shape[1]
    slots = 2 * OWNED

    def one_group(total, inputs):
        group_counts, group_pixels, group_cot = inputs
        ends = jnp.cumsum(group_counts).astype(jnp.int32)
        starts = (ends - group_counts).astype(jnp.int32)
        owner = jnp.arange(n_enc, dtype=jnp.int32)
        place = jnp.arange(OWNED, dtype=jnp.int32)
        global_ids = place[None, :] * n_enc + owner[:, None]
        anchor = jnp.sum((ends[None, None, :] <= global_ids[:, :, None]).astype(jnp.int32), axis=2).astype(jnp.int32)
        within = (global_ids - starts[anchor]).astype(jnp.int32)
        blocks = group_pixels.reshape(n_enc, slots, BLK, PIX)[anchor, within]
        rows = blocks.reshape(n_enc * OWNED * BLK, PIX)
        term = lax.dot_general(group_cot, rows, (((0,), (0,)), ((), ())), preferred_element_type=jnp.float32)
        return total + term, None

    total, _ = lax.scan(one_group, jnp.zeros((D, PIX), jnp.float32), (counts, pixels, cotangent))
    return total
```

```python
import functools

import jax
import jax.numpy as jnp
from jax import lax
from jax.experimental import pallas as pl
from jax.experimental.pallas import tpu as pltpu
from jax.sharding import Mesh
from jax.sharding import PartitionSpec as P

BLK = 16
LANES = 128
TILES = 3
REST = 8
MSG = TILES * BLK + REST
PART = 14
HALF = 44
ENC = ("zh", "y", "x")
Z = ("zh", "zl")


def pack_kernel(me_ref, counts_ref, pix_ref, out_ref, rows_ref):
    n_enc = counts_ref.shape[1]
    patches = pix_ref.shape[1]
    me = me_ref[0]
    start = lax.fori_loop(
        0, n_enc, lambda e, total: total + jnp.where(e < me, counts_ref[0, e], 0), 0
    )
    side = 256
    eye = (
        lax.broadcasted_iota(jnp.int32, (side, side), 0)
        == lax.broadcasted_iota(jnp.int32, (side, side), 1)
    ).astype(jnp.bfloat16)
    for b in range(patches // side):
        turned = lax.dot_general(
            eye,
            pix_ref[: TILES * LANES, b * side : (b + 1) * side],
            (((1,), (1,)), ((), ())),
            preferred_element_type=jnp.float32,
        )
        rows_ref[b * side : (b + 1) * side, :] = turned.astype(jnp.bfloat16)
    for s in range(patches // BLK):
        t = lax.rem(start + s, n_enc)
        for j in range(TILES):
            out_ref[t, j * BLK : (j + 1) * BLK, :] = rows_ref[
                s * BLK : (s + 1) * BLK, j * LANES : (j + 1) * LANES
            ]
        chunk = s * BLK // LANES
        out_ref[t, TILES * BLK :, :] = pix_ref[
            TILES * LANES :, chunk * LANES : (chunk + 1) * LANES
        ]


def grad_kernel(me_ref, counts_ref, arrived_ref, cot_ref, out_ref, rows_ref, rest_ref, sums_ref):
    n_enc = counts_ref.shape[1]
    depth = cot_ref.shape[1]
    me = me_ref[0]
    lane = lax.broadcasted_iota(jnp.int32, (REST, LANES), 1)
    per_tile = LANES // BLK

    def place(e, start):
        count = counts_ref[0, e]
        slot = lax.rem(me - lax.rem(start, n_enc) + n_enc, n_enc)

        @pl.when(slot < count)
        def _():
            k = (start + slot) // n_enc
            to = pl.ds(pl.multiple_of(k * BLK, BLK), BLK)
            for j in range(TILES):
                rows_ref[to, j * LANES : (j + 1) * LANES] = arrived_ref[
                    e, j * BLK : (j + 1) * BLK, :
                ]
            there, here = lax.rem(slot, per_tile), lax.rem(k, per_tile)
            moved = pltpu.roll(
                arrived_ref[e, TILES * BLK :, :].astype(jnp.float32),
                lax.rem(here - there + per_tile, per_tile) * BLK,
                1,
            )
            tile = k // per_tile
            rest_ref[tile] = jnp.where(lane // BLK == here, moved, rest_ref[tile])

        return start + count

    lax.fori_loop(0, n_enc, place, 0)
    rest = jnp.concatenate([rest_ref[i] for i in range(depth // LANES)], axis=1)
    spread = jnp.concatenate([rest] * (LANES // REST), axis=0).astype(jnp.bfloat16)
    step = cot_ref.shape[0] // 4

    def multiply(m, _):
        at = pl.ds(pl.multiple_of(m * step, 16), step)
        cot = cot_ref[at, :]
        sums_ref[at, : TILES * LANES] = jnp.dot(
            cot, rows_ref[...], preferred_element_type=jnp.float32
        )
        sums_ref[at, TILES * LANES :] = lax.dot_general(
            cot, spread, (((1,), (1,)), ((), ())), preferred_element_type=jnp.float32
        )
        return 0

    lax.fori_loop(0, 4, multiply, 0)

    _, nx, ny, _, _ = out_ref.shape
    own = cot_ref.shape[0] // n_enc
    mine = (
        lax.broadcasted_iota(jnp.int32, (PART, LANES), 1) // REST
        == lax.broadcasted_iota(jnp.int32, (PART, LANES), 0)
    )

    def pack(pair, _):
        base = pl.multiple_of(pair * (2 * nx * own), 8)
        for zh in range(2):
            for b in range(2 * nx):
                y, x = pair * 2 + b // nx, b % nx
                for c in range(2):
                    first = zh * nx * ny * own + b * own + c * (own - PART)
                    low = first // 8 * 8
                    span = pl.cdiv(first - low + PART, 8) * 8
                    part = sums_ref[pl.ds(pl.multiple_of(base + low, 8), span), :][
                        first - low : first - low + PART
                    ]
                    for j in range(TILES):
                        out_ref[c, x, y, zh * HALF + j * PART : zh * HALF + (j + 1) * PART, :] = (
                            part[:, j * LANES : (j + 1) * LANES]
                        )
                    rest_row = jnp.sum(
                        jnp.where(mine, part[:, TILES * LANES :], 0.0), axis=0, keepdims=True
                    )
                    out_ref[c, x, y, zh * HALF + TILES * PART : (zh + 1) * HALF, :] = (
                        jnp.broadcast_to(rest_row, (HALF - TILES * PART, LANES))
                    )
        return 0

    lax.fori_loop(0, ny // 2, pack, 0)


def unpack_kernel(parts_ref, out_ref):
    own = out_ref.shape[0]
    for c in range(2):
        first, skip = (0, 0) if c == 0 else (PART, 2 * PART - own)
        for j in range(TILES):
            out_ref[first : first + PART - skip, j * LANES : (j + 1) * LANES] = parts_ref[
                c, j * PART + skip : (j + 1) * PART, :
            ]
        row = parts_ref[c, TILES * PART : TILES * PART + 1, :]
        for r in range(skip, PART):
            out_ref[first + r - skip : first + r - skip + 1, TILES * LANES :] = row[
                :, r * REST : (r + 1) * REST
            ]


def exchange(value, axes):
    return lax.all_to_all(value, axes, split_axis=0, concat_axis=0, tiled=True)


def per_device(counts, pixels, cotangent):
    n_enc = lax.axis_size(ENC)
    nx, ny, nzl = lax.axis_size("x"), lax.axis_size("y"), lax.axis_size("zl")
    me = lax.axis_index(ENC).astype(jnp.int32)[None]
    vmem = pl.BlockSpec(memory_space=pltpu.VMEM)
    smem = pl.BlockSpec(memory_space=pltpu.SMEM)
    pix = pixels[0].T
    cot = cotangent[0].T
    width, depth = cot.shape
    messages = pl.pallas_call(
        pack_kernel,
        out_shape=jax.ShapeDtypeStruct((n_enc, MSG, LANES), jnp.bfloat16),
        in_specs=[smem, smem, vmem],
        out_specs=vmem,
        scratch_shapes=[pltpu.VMEM((pix.shape[1], TILES * LANES), jnp.bfloat16)],
    )(me, counts, pix)
    arrived = exchange(messages, ENC)
    terms = pl.pallas_call(
        grad_kernel,
        out_shape=jax.ShapeDtypeStruct((2, nx, ny, 2 * HALF, LANES), jnp.float32),
        in_specs=[smem, smem, vmem, vmem],
        out_specs=vmem,
        scratch_shapes=[
            pltpu.VMEM((depth, TILES * LANES), jnp.bfloat16),
            pltpu.VMEM((depth // LANES, REST, LANES), jnp.float32),
            pltpu.VMEM((width, (TILES + 1) * LANES), jnp.float32),
        ],
    )(me, counts, arrived, cot)
    terms = jnp.sum(exchange(terms.reshape(2, -1, LANES), "core").reshape(terms.shape), axis=0)
    terms = jnp.sum(exchange(terms.reshape(nx, -1, LANES), "x"), axis=0)
    terms = jnp.sum(exchange(terms.reshape(ny, -1, LANES), "y"), axis=0)
    terms = terms.reshape(2, 1, HALF, LANES)
    terms = jnp.broadcast_to(terms, (2, nzl, HALF, LANES)).reshape(2 * nzl, HALF, LANES)
    terms = jnp.sum(exchange(terms, Z), axis=0)
    parts = exchange(jnp.broadcast_to(terms, (2, HALF, LANES)), "core")
    return pl.pallas_call(
        unpack_kernel,
        out_shape=jax.ShapeDtypeStruct((width // n_enc, pix.shape[0]), jnp.float32),
        in_specs=[vmem],
        out_specs=vmem,
    )(parts)


def solution(mesh):
    torus = Mesh(mesh.devices.reshape(6, 2, 2, 8, 4), ("zl", "core", "zh", "y", "x"))
    dp = ("zl", "core")
    return jax.shard_map(
        per_device,
        mesh=torus,
        in_specs=(P(dp, None), P(dp, ENC, None), P(dp, ENC, None)),
        out_specs=P(ENC, None),
        check_vma=False,
    )
```

```python
import jax
import jax.numpy as jnp
from jax import lax
from jax.experimental import pallas as pl
from jax.experimental.pallas import tpu as pltpu
from jax.sharding import Mesh
from jax.sharding import PartitionSpec as P


BLK = 16
LANES = 128
TILES = 3
REST = 8
MSG = TILES * BLK + REST
PART = 16
HALF = TILES * PART
ENC = ("zh", "y", "x")
Z = ("zh", "zl")
MIB = 1024 * 1024


def pack_kernel(at_ref, counts_ref, pix_ref, out_ref, rows_ref):
    n_enc = counts_ref.shape[1]
    whole, patches = rows_ref.shape[1], pix_ref.shape[1]
    me = at_ref[0]
    start = lax.fori_loop(
        0, n_enc, lambda e, total: total + jnp.where(e < me, counts_ref[0, e], 0), 0
    )
    side = 256
    eye = (
        lax.broadcasted_iota(jnp.int32, (side, side), 0)
        == lax.broadcasted_iota(jnp.int32, (side, side), 1)
    ).astype(jnp.bfloat16)
    for b in range(patches // side):
        turned = lax.dot_general(
            eye,
            pix_ref[:whole, b * side : (b + 1) * side],
            (((1,), (1,)), ((), ())),
            preferred_element_type=jnp.float32,
        )
        rows_ref[b * side : (b + 1) * side, :] = turned.astype(jnp.bfloat16)
    for s in range(patches // BLK):
        t = lax.rem(start + s, n_enc)
        for j in range(TILES):
            out_ref[t, j * BLK : (j + 1) * BLK, :] = rows_ref[
                s * BLK : (s + 1) * BLK, j * LANES : (j + 1) * LANES
            ]
        chunk = s * BLK // LANES
        out_ref[t, TILES * BLK :, :] = pix_ref[whole:, chunk * LANES : (chunk + 1) * LANES]


def cut_kernel(at_ref, cot_ref, *refs):
    *out_refs, wide_ref, cut_ref = refs
    nx, _, rows, _ = cut_ref.shape
    shards = rows // PART
    own = cot_ref.shape[0] // (nx * shards)
    step = cot_ref.shape[0] // 4
    for m in range(4):
        at = slice(m * step, (m + 1) * step)
        wide_ref[at, :] = cot_ref[at, :].astype(jnp.float32)

    def cut(pair, _):
        base = pl.multiple_of(pair * (2 * nx * own), 8)
        for zh in range(2):
            for b in range(2 * nx):
                to = pl.multiple_of(pair * (4 * PART), PART) + (b // nx * 2 + zh) * PART
                for c in range(2):
                    first = zh * nx * (shards // 2) * own + b * own + c * (own - PART)
                    low = first // 8 * 8
                    span = pl.cdiv(first - low + PART, 8) * 8
                    part = wide_ref[pl.ds(pl.multiple_of(base + low, 8), span), :][
                        first - low : first - low + PART
                    ]
                    cut_ref[b % nx, c, pl.ds(pl.multiple_of(to, PART), PART), :] = part.astype(
                        jnp.bfloat16
                    )
        return 0

    lax.fori_loop(0, shards // 4, cut, 0)
    for d, out_ref in enumerate(out_refs):
        out_ref[...] = cut_ref[lax.rem(at_ref[2] + d, nx)]


def place_kernel(at_ref, counts_ref, arrived_ref, out_ref, rest_ref):
    n_enc = counts_ref.shape[1]
    depth = out_ref.shape[1]
    me = at_ref[0]
    lane = lax.broadcasted_iota(jnp.int32, (REST, LANES), 1)
    per_tile = LANES // BLK

    def place(e, start):
        count = counts_ref[0, e]
        slot = lax.rem(me - lax.rem(start, n_enc) + n_enc, n_enc)

        @pl.when(slot < count)
        def _():
            k = (start + slot) // n_enc
            to = pl.ds(pl.multiple_of(k * BLK, BLK), BLK)
            for j in range(TILES):
                out_ref[to, j * LANES : (j + 1) * LANES] = arrived_ref[
                    e, j * BLK : (j + 1) * BLK, :
                ]
            there, here = lax.rem(slot, per_tile), lax.rem(k, per_tile)
            moved = pltpu.roll(
                arrived_ref[e, TILES * BLK :, :].astype(jnp.float32),
                lax.rem(here - there + per_tile, per_tile) * BLK,
                1,
            )
            tile = k // per_tile
            rest_ref[tile] = jnp.where(lane // BLK == here, moved, rest_ref[tile])

        return start + count

    lax.fori_loop(0, n_enc, place, 0)
    rest = jnp.concatenate([rest_ref[i] for i in range(depth // LANES)], axis=1)
    out_ref[depth:, :] = jnp.concatenate([rest, rest], axis=0).astype(jnp.bfloat16)


def grad_kernel(at_ref, *refs):
    keep_ref, send_ref, sums_ref = refs[-3:]
    nx = (len(refs) - 3) // 2
    cut_refs, pix_refs = refs[:nx], refs[nx : 2 * nx]
    rows, depth = cut_refs[0].shape[1:]
    for c in range(2):
        whole = rest = 0.0
        for cut_ref, pix_ref in zip(cut_refs, pix_refs):
            cut = cut_ref[c]
            whole += jnp.dot(cut, pix_ref[:depth, :], preferred_element_type=jnp.float32)
            spread = jnp.concatenate([pix_ref[depth:, :]] * (LANES // (2 * REST)), axis=0)
            rest += lax.dot_general(
                cut, spread, (((1,), (1,)), ((), ())), preferred_element_type=jnp.float32
            )
        sums_ref[c, :, : TILES * LANES] = whole
        sums_ref[c, :, TILES * LANES :] = rest
    place = lax.broadcasted_iota(jnp.int32, (PART, LANES), 0)
    mine = lax.broadcasted_iota(jnp.int32, (PART, LANES), 1) // REST == place
    for out_ref, c in ((keep_ref, at_ref[1]), (send_ref, 1 - at_ref[1])):
        spare = jnp.where(c == 0, PART - 1, 0)
        for q in range(rows // PART):
            y, zh = q // 2, q % 2
            at = slice(q * PART, (q + 1) * PART)
            row = jnp.sum(
                jnp.where(mine, sums_ref[c, at, TILES * LANES :], 0.0), axis=0, keepdims=True
            )
            for j in range(TILES):
                tile = sums_ref[c, at, j * LANES : (j + 1) * LANES]
                if j == 0:
                    tile = jnp.where(place == spare, row, tile)
                out_ref[y, zh * HALF + j * PART : zh * HALF + (j + 1) * PART, :] = tile


def fan_kernel(term_ref, out_ref):
    nz = out_ref.shape[0]
    total = jnp.sum(term_ref[...], axis=0)
    for z in range(nz):
        zh = z // (nz // 2)
        out_ref[z] = total[zh * HALF : (zh + 1) * HALF]


def unpack_kernel(parts_ref, out_ref):
    own = out_ref.shape[0]
    cut = own // 2 + 1
    for c, low, high, first in ((0, 0, cut, 0), (1, cut, own, own - PART)):
        for j in range(TILES):
            out_ref[low:high, j * LANES : (j + 1) * LANES] = parts_ref[
                c, j * PART + low - first : j * PART + high - first, :
            ]
        spare = PART - 1 if c == 0 else 0
        row = parts_ref[c, spare : spare + 1, :]
        for r in range(low, high):
            out_ref[r : r + 1, TILES * LANES :] = row[:, (r - first) * REST : (r - first + 1) * REST]


def exchange(value, axes):
    return lax.all_to_all(value, axes, split_axis=0, concat_axis=0, tiled=True)


def shift(value, axis, by):
    size = lax.axis_size(axis)
    return lax.ppermute(value, axis, [(i, (i + by) % size) for i in range(size)])


def call(kernel, out_shape, scratch, args, scalars, mib):
    spaces = [pltpu.SMEM] * scalars + [pltpu.VMEM] * (len(args) - scalars)
    return pl.pallas_call(
        kernel,
        out_shape=out_shape,
        in_specs=[pl.BlockSpec(memory_space=space) for space in spaces],
        out_specs=jax.tree.map(lambda _: pl.BlockSpec(memory_space=pltpu.VMEM), out_shape),
        scratch_shapes=scratch,
        compiler_params=pltpu.CompilerParams(vmem_limit_bytes=mib * MIB),
        cost_estimate=pl.CostEstimate(flops=0, bytes_accessed=6 * MIB, transcendentals=0),
    )(*args)


def gradient(counts, pixels, cotangent):
    n_enc = lax.axis_size(ENC)
    nx, ny, nzl = lax.axis_size("x"), lax.axis_size("y"), lax.axis_size("zl")
    at = jnp.stack([lax.axis_index(ENC), lax.axis_index("core"), lax.axis_index("x")])
    at = at.astype(jnp.int32)
    pix, cot = pixels[0].T, cotangent[0].T
    width, depth = cot.shape
    bf16 = lambda *shape: jax.ShapeDtypeStruct(shape, jnp.bfloat16)
    f32 = lambda *shape: jax.ShapeDtypeStruct(shape, jnp.float32)
    rows = 2 * ny * PART

    messages = call(
        pack_kernel,
        bf16(n_enc, MSG, LANES),
        [pltpu.VMEM((pix.shape[1], TILES * LANES), jnp.bfloat16)],
        (at, counts, pix),
        2,
        8,
    )
    arrived = exchange(messages, ENC)
    cuts = call(
        cut_kernel,
        [bf16(2, rows, depth)] * nx,
        [pltpu.VMEM((width, depth), jnp.float32), pltpu.VMEM((nx, 2, rows, depth), jnp.bfloat16)],
        (at, cot),
        1,
        12,
    )
    cuts = [cuts[0]] + [shift(cuts[d], "x", d) for d in range(1, nx)]
    placed = call(
        place_kernel,
        bf16(depth + 2 * REST, TILES * LANES),
        [pltpu.VMEM((depth // LANES, REST, LANES), jnp.float32)],
        (at, counts, arrived),
        2,
        8,
    )
    row = [placed] + [shift(placed, "x", d) for d in range(1, nx)]
    keep, send = call(
        grad_kernel,
        [f32(ny, 2 * HALF, LANES)] * 2,
        [pltpu.VMEM((2, rows, (TILES + 1) * LANES), jnp.float32)],
        (at, *cuts, *row),
        1,
        16,
    )
    terms = keep + shift(send, "core", 1)
    terms = exchange(terms, "y")
    terms = call(fan_kernel, f32(2 * nzl, HALF, LANES), [], (terms,), 0, 8)
    terms = jnp.sum(exchange(terms, Z), axis=0)
    parts = exchange(jnp.broadcast_to(terms, (2, HALF, LANES)), "core")
    return call(unpack_kernel, f32(width // n_enc, pix.shape[0]), [], (parts,), 0, 8)


def solution(mesh):
    torus = Mesh(mesh.devices.reshape(6, 2, 2, 8, 4), ("zl", "core", "zh", "y", "x"))
    dp = ("zl", "core")
    return jax.shard_map(
        gradient,
        mesh=torus,
        in_specs=(P(dp, None), P(dp, ENC, None), P(dp, ENC, None)),
        out_specs=P(ENC, None),
        check_vma=False,
    )
```

```python
import jax
import jax.numpy as jnp
from jax import lax
from jax.experimental import pallas as pl
from jax.experimental.pallas import tpu as pltpu
from jax.sharding import Mesh
from jax.sharding import PartitionSpec as P


BLK = 16
LANES = 128
TILES = 3
REST = 8
PAIRS = TILES * BLK // 2 + 1
PART = 16
HALF = TILES * PART
ENC = ("zh", "y", "x")
Z = ("zh", "zl")
DP = ("zl", "core")
FIRST = 3
MIB = 1024 * 1024


def pack_kernel(at_ref, pix_ref, out_ref, rows_ref):
    n_enc = out_ref.shape[0]
    whole, patches = rows_ref.shape[1], pix_ref.shape[1]
    me = at_ref[0]
    start = lax.fori_loop(
        0,
        n_enc,
        lambda e, total: total + jnp.where(e < me, at_ref[FIRST + e], 0),
        0,
        unroll=8,
    )
    side = 256
    eye = (
        lax.broadcasted_iota(jnp.int32, (side, side), 0)
        == lax.broadcasted_iota(jnp.int32, (side, side), 1)
    ).astype(jnp.bfloat16)
    for b in range(patches // side):
        turned = lax.dot_general(
            eye,
            pix_ref[:whole, b * side : (b + 1) * side],
            (((1,), (1,)), ((), ())),
            preferred_element_type=jnp.float32,
        )
        rows_ref[b * side : (b + 1) * side, :] = turned.astype(jnp.bfloat16)
    column = lax.broadcasted_iota(jnp.int32, (REST, LANES), 0)
    mine = lax.broadcasted_iota(jnp.int32, (REST, LANES), 1) // BLK == column
    per_tile = LANES // BLK
    rests = []
    for tile in range(patches // LANES):
        rest = pix_ref[whole:, tile * LANES : (tile + 1) * LANES].astype(jnp.float32)
        rests.append(pltpu.roll(rest, 0, 1, stride=BLK, stride_axis=0))
    for s in range(patches // BLK):
        t = lax.rem(start + s, n_enc)
        for j in range(TILES):
            block = rows_ref[s * BLK : (s + 1) * BLK, j * LANES : (j + 1) * LANES]
            out_ref[t, j * BLK // 2 : (j + 1) * BLK // 2] = block.reshape(BLK // 2, 2, LANES)
        rest = pltpu.roll(rests[s // per_tile], -s % per_tile * BLK, 1)
        row = jnp.sum(jnp.where(mine, rest, 0.0), axis=0, keepdims=True)
        out_ref[t, PAIRS - 1] = jnp.broadcast_to(row, (2, LANES)).astype(jnp.bfloat16)


def cut_kernel(at_ref, cot_ref, *refs):
    *out_refs, from_ref, wide_ref, cut_ref = refs
    nx, _, rows, _ = cut_ref.shape
    shards = rows // PART
    own = cot_ref.shape[0] // (nx * shards)
    step = cot_ref.shape[0] // 4
    for m in range(4):
        at = slice(m * step, (m + 1) * step)
        wide_ref[at, :] = cot_ref[at, :].astype(jnp.float32)

    def cut(pair, _):
        base = pl.multiple_of(pair * (2 * nx * own), 8)
        for zh in range(2):
            for b in range(2 * nx):
                to = pl.multiple_of(pair * (4 * PART), PART) + (b // nx * 2 + zh) * PART
                for c in range(2):
                    first = zh * nx * (shards // 2) * own + b * own + c * (own - PART)
                    low = first // 8 * 8
                    span = pl.cdiv(first - low + PART, 8) * 8
                    part = wide_ref[pl.ds(pl.multiple_of(base + low, 8), span), :][
                        first - low : first - low + PART
                    ]
                    cut_ref[b % nx, c, pl.ds(pl.multiple_of(to, PART), PART), :] = part.astype(
                        jnp.bfloat16
                    )
        return 0

    lax.fori_loop(0, shards // 4, cut, 0)
    for d, out_ref in enumerate(out_refs):
        out_ref[...] = cut_ref[lax.rem(at_ref[2] + d, nx)]
    n_enc = nx * shards

    def trace(e, start):
        count = at_ref[FIRST + e]
        slot = lax.rem(at_ref[0] - lax.rem(start, n_enc) + n_enc, n_enc)

        @pl.when(slot < count)
        def _():
            from_ref[(start + slot) // n_enc] = e

        return start + count

    lax.fori_loop(0, n_enc, trace, 0)


def place_kernel(from_ref, arrived_ref, out_ref):
    depth = out_ref.shape[1]
    column = lax.broadcasted_iota(jnp.int32, (REST, LANES), 0)
    lane = lax.broadcasted_iota(jnp.int32, (REST, LANES), 1)
    per_tile = LANES // BLK
    rests = []
    for k in range(depth // BLK):
        e = from_ref[k]
        for j in range(TILES):
            block = arrived_ref[e, j * BLK // 2 : (j + 1) * BLK // 2]
            out_ref[k * BLK : (k + 1) * BLK, j * LANES : (j + 1) * LANES] = block.reshape(
                BLK, LANES
            )
        row = arrived_ref[e, PAIRS - 1].astype(jnp.float32)[:1]
        here = k % per_tile
        moved = pltpu.roll(jnp.broadcast_to(row, (REST, LANES)), here * BLK, 1)
        for by in (1, 2, 4):
            back = pltpu.roll(moved, LANES - by * BLK, 1)
            moved = jnp.where(column // by % 2 == 1, back, moved)
        if here == 0:
            rests.append(moved)
        else:
            rests[-1] = jnp.where(lane // BLK == here, moved, rests[-1])
    rest = jnp.concatenate(rests, axis=1)
    out_ref[depth:, :] = jnp.concatenate([rest, rest], axis=0).astype(jnp.bfloat16)


def grad_kernel(at_ref, *refs):
    keep_ref, send_ref, sums_ref = refs[-3:]
    nx = (len(refs) - 3) // 2
    cut_refs, pix_refs = refs[:nx], refs[nx : 2 * nx]
    rows, depth = cut_refs[0].shape[1:]
    for c in range(2):
        whole = rest = 0.0
        for cut_ref, pix_ref in zip(cut_refs, pix_refs):
            cut = cut_ref[c]
            whole += jnp.dot(cut, pix_ref[:depth, :], preferred_element_type=jnp.float32)
            spread = jnp.concatenate([pix_ref[depth:, :]] * (LANES // (2 * REST)), axis=0)
            rest += lax.dot_general(
                cut, spread, (((1,), (1,)), ((), ())), preferred_element_type=jnp.float32
            )
        sums_ref[c, :, : TILES * LANES] = whole
        sums_ref[c, :, TILES * LANES :] = rest
    place = lax.broadcasted_iota(jnp.int32, (PART, LANES), 0)
    mine = lax.broadcasted_iota(jnp.int32, (PART, LANES), 1) // REST == place
    for out_ref, c in ((keep_ref, at_ref[1]), (send_ref, 1 - at_ref[1])):
        spare = jnp.where(c == 0, PART - 1, 0)
        for q in range(rows // PART):
            y, zh = q // 2, q % 2
            at = slice(q * PART, (q + 1) * PART)
            row = jnp.sum(
                jnp.where(mine, sums_ref[c, at, TILES * LANES :], 0.0), axis=0, keepdims=True
            )
            for j in range(TILES):
                tile = sums_ref[c, at, j * LANES : (j + 1) * LANES]
                if j == 0:
                    tile = jnp.where(place == spare, row, tile)
                out_ref[y, zh * HALF + j * PART : zh * HALF + (j + 1) * PART, :] = tile


def unpack_kernel(parts_ref, out_ref):
    own = out_ref.shape[0]
    cut = own // 2 + 1
    for c, low, high, first in ((0, 0, cut, 0), (1, cut, own, own - PART)):
        for j in range(TILES):
            tile = jnp.concatenate([parts_ref[4 * j + c], parts_ref[4 * j + 2 + c]], axis=0)
            out_ref[low:high, j * LANES : (j + 1) * LANES] = tile[low - first : high - first]
            if j == 0:
                spare = PART - 1 if c == 0 else 0
                row = tile[spare : spare + 1]
        for r in range(low, high):
            out_ref[r : r + 1, TILES * LANES :] = row[:, (r - first) * REST : (r - first + 1) * REST]


def exchange(value, axes):
    return lax.all_to_all(value, axes, split_axis=0, concat_axis=0, tiled=True)


def shift(value, axis, by):
    size = lax.axis_size(axis)
    return lax.ppermute(value, axis, [(i, (i + by) % size) for i in range(size)])


def call(kernel, out_shape, scratch, args, mib):
    spaces = [pltpu.SMEM if a.dtype == jnp.int32 else pltpu.VMEM for a in args]
    outs = jax.tree.map(
        lambda o: pl.BlockSpec(memory_space=pltpu.SMEM if o.dtype == jnp.int32 else pltpu.VMEM),
        out_shape,
    )
    return pl.pallas_call(
        kernel,
        out_shape=out_shape,
        in_specs=[pl.BlockSpec(memory_space=space) for space in spaces],
        out_specs=outs,
        scratch_shapes=scratch,
        compiler_params=pltpu.CompilerParams(vmem_limit_bytes=mib * MIB),
        cost_estimate=pl.CostEstimate(flops=0, bytes_accessed=6 * MIB, transcendentals=0),
    )(*args)


def gradient(counts, pixels, cotangent):
    n_enc, n_dp, nz = lax.axis_size(ENC), lax.axis_size(DP), lax.axis_size(Z)
    nx, ny = lax.axis_size("x"), lax.axis_size("y")
    at = [lax.axis_index(ENC), lax.axis_index("core"), lax.axis_index("x")]
    at = jnp.concatenate([jnp.stack(at).astype(jnp.int32), counts[0]])
    pix, cot = pixels[0].T, cotangent[0].T
    width, depth = cot.shape
    bf16 = lambda *shape: jax.ShapeDtypeStruct(shape, jnp.bfloat16)
    f32 = lambda *shape: jax.ShapeDtypeStruct(shape, jnp.float32)
    rows = 2 * ny * PART

    messages = call(
        pack_kernel,
        bf16(n_enc, PAIRS, 2, LANES),
        [pltpu.VMEM((pix.shape[1], TILES * LANES), jnp.bfloat16)],
        (at, pix),
        8,
    )
    arrived = exchange(messages, ENC)
    *cuts, source = call(
        cut_kernel,
        [bf16(2, rows, depth)] * nx + [jax.ShapeDtypeStruct((depth // BLK,), jnp.int32)],
        [pltpu.VMEM((width, depth), jnp.float32), pltpu.VMEM((nx, 2, rows, depth), jnp.bfloat16)],
        (at, cot),
        12,
    )
    cuts = [cuts[0]] + [shift(cuts[d], "x", d) for d in range(1, nx)]
    placed = call(
        place_kernel, bf16(depth + 2 * REST, TILES * LANES), [], (source, arrived), 8
    )
    row = [placed] + [shift(placed, "x", d) for d in range(1, nx)]
    keep, send = call(
        grad_kernel,
        [f32(ny, 2 * HALF, LANES)] * 2,
        [pltpu.VMEM((2, rows, (TILES + 1) * LANES), jnp.float32)],
        (at, *cuts, *row),
        16,
    )
    terms = keep + shift(send, "core", 1)
    terms = jnp.sum(exchange(terms, "y"), axis=0)
    terms = jnp.sum(exchange(terms.reshape(nz, -1, LANES), Z), axis=0)
    parts = exchange(jnp.broadcast_to(terms, (n_dp, *terms.shape)), DP)
    return call(unpack_kernel, f32(width // n_enc, pix.shape[0]), [], (parts,), 8)


def solution(mesh):
    torus = Mesh(mesh.devices.reshape(6, 2, 2, 8, 4), ("zl", "core", "zh", "y", "x"))
    return jax.shard_map(
        gradient,
        mesh=torus,
        in_specs=(P(DP, None), P(DP, ENC, None), P(DP, ENC, None)),
        out_specs=P(ENC, None),
        check_vma=False,
    )
```

```python
import jax
import jax.numpy as jnp
from jax import lax
from jax.experimental import pallas as pl
from jax.experimental.pallas import tpu as pltpu
from jax.sharding import Mesh
from jax.sharding import PartitionSpec as P


BLK = 16
LANES = 128
TILES = 3
REST = 8
PAIRS = TILES * BLK // 2 + 1
PART = 16
HALF = TILES * PART
ENC = ("zh", "y", "x")
Z = ("zh", "zl")
DP = ("zl", "core")
FIRST = 3
MIB = 1024 * 1024


def pack_kernel(at_ref, pix_ref, out_ref, rows_ref):
    n_enc = out_ref.shape[0]
    whole, patches = rows_ref.shape[1], pix_ref.shape[1]
    me = at_ref[0]
    start = lax.fori_loop(
        0,
        n_enc,
        lambda e, total: total + jnp.where(e < me, at_ref[FIRST + e], 0),
        0,
        unroll=8,
    )
    side = 256
    eye = (
        lax.broadcasted_iota(jnp.int32, (side, side), 0)
        == lax.broadcasted_iota(jnp.int32, (side, side), 1)
    ).astype(jnp.bfloat16)
    for b in range(patches // side):
        turned = lax.dot_general(
            eye,
            pix_ref[:whole, b * side : (b + 1) * side],
            (((1,), (1,)), ((), ())),
            preferred_element_type=jnp.float32,
        )
        rows_ref[b * side : (b + 1) * side, :] = turned.astype(jnp.bfloat16)
    column = lax.broadcasted_iota(jnp.int32, (REST, LANES), 0)
    mine = lax.broadcasted_iota(jnp.int32, (REST, LANES), 1) // BLK == column
    per_tile = LANES // BLK
    rests = []
    for tile in range(patches // LANES):
        rest = pix_ref[whole:, tile * LANES : (tile + 1) * LANES].astype(jnp.float32)
        rests.append(pltpu.roll(rest, 0, 1, stride=BLK, stride_axis=0))
    for s in range(patches // BLK):
        t = lax.rem(start + s, n_enc)
        for j in range(TILES):
            block = rows_ref[s * BLK : (s + 1) * BLK, j * LANES : (j + 1) * LANES]
            out_ref[t, j * BLK // 2 : (j + 1) * BLK // 2] = block.reshape(BLK // 2, 2, LANES)
        rest = pltpu.roll(rests[s // per_tile], -s % per_tile * BLK, 1)
        row = jnp.sum(jnp.where(mine, rest, 0.0), axis=0, keepdims=True)
        out_ref[t, PAIRS - 1] = jnp.broadcast_to(row, (2, LANES)).astype(jnp.bfloat16)


def cut_kernel(at_ref, cot_ref, *refs):
    *out_refs, wide_ref, cut_ref = refs
    nx, _, rows, _ = cut_ref.shape
    shards = rows // PART
    own = cot_ref.shape[0] // (nx * shards)
    step = cot_ref.shape[0] // 4
    for m in range(4):
        at = slice(m * step, (m + 1) * step)
        wide_ref[at, :] = cot_ref[at, :].astype(jnp.float32)

    def cut(pair, _):
        base = pl.multiple_of(pair * (2 * nx * own), 8)
        for zh in range(2):
            for b in range(2 * nx):
                to = pl.multiple_of(pair * (4 * PART), PART) + (b // nx * 2 + zh) * PART
                for c in range(2):
                    first = zh * nx * (shards // 2) * own + b * own + c * (own - PART)
                    low = first // 8 * 8
                    span = pl.cdiv(first - low + PART, 8) * 8
                    part = wide_ref[pl.ds(pl.multiple_of(base + low, 8), span), :][
                        first - low : first - low + PART
                    ]
                    cut_ref[b % nx, c, pl.ds(pl.multiple_of(to, PART), PART), :] = part.astype(
                        jnp.bfloat16
                    )
        return 0

    lax.fori_loop(0, shards // 4, cut, 0)
    for d, out_ref in enumerate(out_refs):
        out_ref[...] = cut_ref[lax.rem(at_ref[2] + d, nx)]


def trace_kernel(at_ref, from_ref):
    n_enc = at_ref.shape[0] - FIRST

    def trace(e, start):
        count = at_ref[FIRST + e]
        slot = lax.rem(at_ref[0] - lax.rem(start, n_enc) + n_enc, n_enc)

        @pl.when(slot < count)
        def _():
            from_ref[(start + slot) // n_enc] = e

        return start + count

    lax.fori_loop(0, n_enc, trace, 0)


def place_kernel(from_ref, arrived_ref, out_ref):
    depth = out_ref.shape[2]
    column = lax.broadcasted_iota(jnp.int32, (REST, LANES), 0)
    lane = lax.broadcasted_iota(jnp.int32, (REST, LANES), 1)
    per_tile = LANES // BLK
    rests = []
    for k in range(depth // BLK):
        e = from_ref[k]
        for j in range(TILES):
            block = arrived_ref[e, j * BLK // 2 : (j + 1) * BLK // 2]
            out_ref[0, k * BLK : (k + 1) * BLK, j * LANES : (j + 1) * LANES] = block.reshape(
                BLK, LANES
            )
        row = arrived_ref[e, PAIRS - 1].astype(jnp.float32)[:1]
        here = k % per_tile
        moved = pltpu.roll(jnp.broadcast_to(row, (REST, LANES)), here * BLK, 1)
        for by in (1, 2, 4):
            back = pltpu.roll(moved, LANES - by * BLK, 1)
            moved = jnp.where(column // by % 2 == 1, back, moved)
        if here == 0:
            rests.append(moved)
        else:
            rests[-1] = jnp.where(lane // BLK == here, moved, rests[-1])
    rest = jnp.concatenate(rests, axis=1)
    out_ref[0, depth:, :] = jnp.concatenate([rest, rest], axis=0).astype(jnp.bfloat16)
    for i in range(1, out_ref.shape[0]):
        out_ref[i] = out_ref[0]


def grad_kernel(at_ref, *refs):
    keep_ref, send_ref, sums_ref = refs[-3:]
    *cut_refs, pix_ref = refs[:-3]
    nx = len(cut_refs)
    rows, depth = cut_refs[0].shape[1:]
    for c in range(2):
        whole = rest = 0.0
        for d, cut_ref in enumerate(cut_refs):
            came = lax.rem(at_ref[2] + nx - d, nx)
            cut = cut_ref[c]
            whole += jnp.dot(cut, pix_ref[came, :depth, :], preferred_element_type=jnp.float32)
            spread = jnp.concatenate([pix_ref[came, depth:, :]] * (LANES // (2 * REST)), axis=0)
            rest += lax.dot_general(
                cut, spread, (((1,), (1,)), ((), ())), preferred_element_type=jnp.float32
            )
        sums_ref[c, :, : TILES * LANES] = whole
        sums_ref[c, :, TILES * LANES :] = rest
    place = lax.broadcasted_iota(jnp.int32, (PART, LANES), 0)
    mine = lax.broadcasted_iota(jnp.int32, (PART, LANES), 1) // REST == place
    for out_ref, c in ((keep_ref, at_ref[1]), (send_ref, 1 - at_ref[1])):
        spare = jnp.where(c == 0, PART - 1, 0)
        for q in range(rows // PART):
            y, zh = q // 2, q % 2
            at = slice(q * PART, (q + 1) * PART)
            row = jnp.sum(
                jnp.where(mine, sums_ref[c, at, TILES * LANES :], 0.0), axis=0, keepdims=True
            )
            for j in range(TILES):
                tile = sums_ref[c, at, j * LANES : (j + 1) * LANES]
                if j == 0:
                    tile = jnp.where(place == spare, row, tile)
                out_ref[y, zh * HALF + j * PART : zh * HALF + (j + 1) * PART, :] = tile


def unpack_kernel(parts_ref, out_ref):
    own = out_ref.shape[0]
    cut = own // 2 + 1
    for c, low, high, first in ((0, 0, cut, 0), (1, cut, own, own - PART)):
        for j in range(TILES):
            tile = jnp.concatenate([parts_ref[4 * j + c], parts_ref[4 * j + 2 + c]], axis=0)
            out_ref[low:high, j * LANES : (j + 1) * LANES] = tile[low - first : high - first]
            if j == 0:
                spare = PART - 1 if c == 0 else 0
                row = tile[spare : spare + 1]
        for r in range(low, high):
            out_ref[r : r + 1, TILES * LANES :] = row[:, (r - first) * REST : (r - first + 1) * REST]


def exchange(value, axes):
    return lax.all_to_all(value, axes, split_axis=0, concat_axis=0, tiled=True)


def shift(value, axis, by):
    size = lax.axis_size(axis)
    return lax.ppermute(value, axis, [(i, (i + by) % size) for i in range(size)])


def call(kernel, out_shape, scratch, args, mib):
    spaces = [pltpu.SMEM if a.dtype == jnp.int32 else pltpu.VMEM for a in args]
    outs = jax.tree.map(
        lambda o: pl.BlockSpec(memory_space=pltpu.SMEM if o.dtype == jnp.int32 else pltpu.VMEM),
        out_shape,
    )
    return pl.pallas_call(
        kernel,
        out_shape=out_shape,
        in_specs=[pl.BlockSpec(memory_space=space) for space in spaces],
        out_specs=outs,
        scratch_shapes=scratch,
        compiler_params=pltpu.CompilerParams(vmem_limit_bytes=mib * MIB),
        cost_estimate=pl.CostEstimate(flops=0, bytes_accessed=6 * MIB, transcendentals=0),
    )(*args)


def gradient(counts, pixels, cotangent):
    n_enc, n_dp, nz = lax.axis_size(ENC), lax.axis_size(DP), lax.axis_size(Z)
    nx, ny = lax.axis_size("x"), lax.axis_size("y")
    at = [lax.axis_index(ENC), lax.axis_index("core"), lax.axis_index("x")]
    at = jnp.concatenate([jnp.stack(at).astype(jnp.int32), counts[0]])
    pix, cot = pixels[0].T, cotangent[0].T
    width, depth = cot.shape
    bf16 = lambda *shape: jax.ShapeDtypeStruct(shape, jnp.bfloat16)
    f32 = lambda *shape: jax.ShapeDtypeStruct(shape, jnp.float32)
    rows = 2 * ny * PART

    messages = call(
        pack_kernel,
        bf16(n_enc, PAIRS, 2, LANES),
        [pltpu.VMEM((pix.shape[1], TILES * LANES), jnp.bfloat16)],
        (at, pix),
        8,
    )
    arrived = exchange(messages, ENC)
    cuts = call(
        cut_kernel,
        [bf16(2, rows, depth)] * nx,
        [pltpu.VMEM((width, depth), jnp.float32), pltpu.VMEM((nx, 2, rows, depth), jnp.bfloat16)],
        (at, cot),
        12,
    )
    cuts = [cuts[0]] + [shift(cuts[d], "x", d) for d in range(1, nx)]
    source = call(trace_kernel, jax.ShapeDtypeStruct((depth // BLK,), jnp.int32), [], (at,), 1)
    placed = call(place_kernel, bf16(nx, depth + 2 * REST, TILES * LANES), [], (source, arrived), 8)
    placed, cuts = lax.optimization_barrier((placed, cuts))
    row = exchange(placed, "x")
    keep, send = call(
        grad_kernel,
        [f32(ny, 2 * HALF, LANES)] * 2,
        [pltpu.VMEM((2, rows, (TILES + 1) * LANES), jnp.float32)],
        (at, *cuts, row),
        16,
    )
    terms = keep + shift(send, "core", 1)
    terms = jnp.sum(exchange(terms.reshape(ny * nz, -1, LANES), ("y", *Z)), axis=0)
    parts = exchange(jnp.broadcast_to(terms, (n_dp, *terms.shape)), DP)
    return call(unpack_kernel, f32(width // n_enc, pix.shape[0]), [], (parts,), 8)


def solution(mesh):
    torus = Mesh(mesh.devices.reshape(6, 2, 2, 8, 4), ("zl", "core", "zh", "y", "x"))
    return jax.shard_map(
        gradient,
        mesh=torus,
        in_specs=(P(DP, None), P(DP, ENC, None), P(DP, ENC, None)),
        out_specs=P(ENC, None),
        check_vma=False,
    )
```

```python
import jax
import jax.numpy as jnp
from jax import lax
from jax.experimental import pallas as pl
from jax.experimental.pallas import tpu as pltpu
from jax.sharding import Mesh
from jax.sharding import PartitionSpec as P


BLK = 16
LANES = 128
TILES = 3
REST = 8
PAIRS = TILES * BLK // 2 + 1
PART = 16
HALF = TILES * PART
ENC = ("zh", "y", "x")
Z = ("zh", "zl")
DP = ("zl", "core")
FIRST = 3
MIB = 1024 * 1024


def pack_kernel(me_ref, counts_ref, far_ref, out_ref, rows_ref, pix_ref, sems):
    n_enc = out_ref.shape[0]
    whole, patches = rows_ref.shape[1], pix_ref.shape[1]
    side = 256
    copies = [
        pltpu.make_async_copy(
            far_ref.at[:, b * side : (b + 1) * side],
            pix_ref.at[:, b * side : (b + 1) * side],
            sems.at[b],
        )
        for b in range(patches // side)
    ]
    for copy in copies:
        copy.start()
    me = me_ref[0]
    start = lax.fori_loop(
        0,
        n_enc,
        lambda e, total: total + jnp.where(e < me, counts_ref[0, e], 0),
        0,
        unroll=8,
    )
    eye = (
        lax.broadcasted_iota(jnp.int32, (side, side), 0)
        == lax.broadcasted_iota(jnp.int32, (side, side), 1)
    ).astype(jnp.bfloat16)
    for b in range(patches // side):
        copies[b].wait()
        turned = lax.dot_general(
            eye,
            pix_ref[:whole, b * side : (b + 1) * side],
            (((1,), (1,)), ((), ())),
            preferred_element_type=jnp.float32,
        )
        rows_ref[b * side : (b + 1) * side, :] = turned.astype(jnp.bfloat16)
    column = lax.broadcasted_iota(jnp.int32, (REST, LANES), 0)
    mine = lax.broadcasted_iota(jnp.int32, (REST, LANES), 1) // BLK == column
    per_tile = LANES // BLK
    rests = []
    for tile in range(patches // LANES):
        rest = pix_ref[whole:, tile * LANES : (tile + 1) * LANES].astype(jnp.float32)
        rests.append(pltpu.roll(rest, 0, 1, stride=BLK, stride_axis=0))
    for s in range(patches // BLK):
        t = lax.rem(start + s, n_enc)
        for j in range(TILES):
            block = rows_ref[s * BLK : (s + 1) * BLK, j * LANES : (j + 1) * LANES]
            out_ref[t, j * BLK // 2 : (j + 1) * BLK // 2] = block.reshape(BLK // 2, 2, LANES)
        rest = pltpu.roll(rests[s // per_tile], -s % per_tile * BLK, 1)
        row = jnp.sum(jnp.where(mine, rest, 0.0), axis=0, keepdims=True)
        out_ref[t, PAIRS - 1] = jnp.broadcast_to(row, (2, LANES)).astype(jnp.bfloat16)


def cut_kernel(at_ref, cot_ref, *refs):
    *out_refs, wide_ref, cut_ref = refs
    nx, _, rows, _ = cut_ref.shape
    shards = rows // PART
    own = cot_ref.shape[0] // (nx * shards)
    step = cot_ref.shape[0] // 4
    for m in range(4):
        at = slice(m * step, (m + 1) * step)
        wide_ref[at, :] = cot_ref[at, :].astype(jnp.float32)

    def cut(pair, _):
        base = pl.multiple_of(pair * (2 * nx * own), 8)
        for zh in range(2):
            for b in range(2 * nx):
                to = pl.multiple_of(pair * (4 * PART), PART) + (b // nx * 2 + zh) * PART
                for c in range(2):
                    first = zh * nx * (shards // 2) * own + b * own + c * (own - PART)
                    low = first // 8 * 8
                    span = pl.cdiv(first - low + PART, 8) * 8
                    part = wide_ref[pl.ds(pl.multiple_of(base + low, 8), span), :][
                        first - low : first - low + PART
                    ]
                    cut_ref[b % nx, c, pl.ds(pl.multiple_of(to, PART), PART), :] = part.astype(
                        jnp.bfloat16
                    )
        return 0

    lax.fori_loop(0, shards // 4, cut, 0)
    for d, out_ref in enumerate(out_refs):
        out_ref[...] = cut_ref[lax.rem(at_ref[2] + d, nx)]


def trace_kernel(at_ref, from_ref):
    n_enc = at_ref.shape[0] - FIRST

    def trace(e, start):
        count = at_ref[FIRST + e]
        slot = lax.rem(at_ref[0] - lax.rem(start, n_enc) + n_enc, n_enc)

        @pl.when(slot < count)
        def _():
            from_ref[(start + slot) // n_enc] = e

        return start + count

    lax.fori_loop(0, n_enc, trace, 0)


def place_kernel(from_ref, arrived_ref, out_ref):
    depth = out_ref.shape[2]
    column = lax.broadcasted_iota(jnp.int32, (REST, LANES), 0)
    lane = lax.broadcasted_iota(jnp.int32, (REST, LANES), 1)
    per_tile = LANES // BLK
    rests = []
    for k in range(depth // BLK):
        e = from_ref[k]
        for j in range(TILES):
            block = arrived_ref[e, j * BLK // 2 : (j + 1) * BLK // 2]
            out_ref[0, k * BLK : (k + 1) * BLK, j * LANES : (j + 1) * LANES] = block.reshape(
                BLK, LANES
            )
        row = arrived_ref[e, PAIRS - 1].astype(jnp.float32)[:1]
        here = k % per_tile
        moved = pltpu.roll(jnp.broadcast_to(row, (REST, LANES)), here * BLK, 1)
        for by in (1, 2, 4):
            back = pltpu.roll(moved, LANES - by * BLK, 1)
            moved = jnp.where(column // by % 2 == 1, back, moved)
        if here == 0:
            rests.append(moved)
        else:
            rests[-1] = jnp.where(lane // BLK == here, moved, rests[-1])
    rest = jnp.concatenate(rests, axis=1)
    out_ref[0, depth:, :] = jnp.concatenate([rest, rest], axis=0).astype(jnp.bfloat16)
    for i in range(1, out_ref.shape[0]):
        out_ref[i] = out_ref[0]


def grad_kernel(at_ref, *refs):
    keep_ref, send_ref, sums_ref = refs[-3:]
    *cut_refs, pix_ref = refs[:-3]
    nx = len(cut_refs)
    rows, depth = cut_refs[0].shape[1:]
    for c in range(2):
        whole = rest = 0.0
        for d, cut_ref in enumerate(cut_refs):
            came = lax.rem(at_ref[2] + nx - d, nx)
            cut = cut_ref[c]
            whole += jnp.dot(cut, pix_ref[came, :depth, :], preferred_element_type=jnp.float32)
            spread = jnp.concatenate([pix_ref[came, depth:, :]] * (LANES // (2 * REST)), axis=0)
            rest += lax.dot_general(
                cut, spread, (((1,), (1,)), ((), ())), preferred_element_type=jnp.float32
            )
        sums_ref[c, :, : TILES * LANES] = whole
        sums_ref[c, :, TILES * LANES :] = rest
    place = lax.broadcasted_iota(jnp.int32, (PART, LANES), 0)
    mine = lax.broadcasted_iota(jnp.int32, (PART, LANES), 1) // REST == place
    for out_ref, c in ((keep_ref, at_ref[1]), (send_ref, 1 - at_ref[1])):
        spare = jnp.where(c == 0, PART - 1, 0)
        for q in range(rows // PART):
            y, zh = q // 2, q % 2
            at = slice(q * PART, (q + 1) * PART)
            row = jnp.sum(
                jnp.where(mine, sums_ref[c, at, TILES * LANES :], 0.0), axis=0, keepdims=True
            )
            for j in range(TILES):
                tile = sums_ref[c, at, j * LANES : (j + 1) * LANES]
                if j == 0:
                    tile = jnp.where(place == spare, row, tile)
                out_ref[y, zh * HALF + j * PART : zh * HALF + (j + 1) * PART, :] = tile


def unpack_kernel(parts_ref, out_ref):
    own = out_ref.shape[0]
    cut = own // 2 + 1
    for c, low, high, first in ((0, 0, cut, 0), (1, cut, own, own - PART)):
        for j in range(TILES):
            tile = jnp.concatenate([parts_ref[4 * j + c], parts_ref[4 * j + 2 + c]], axis=0)
            out_ref[low:high, j * LANES : (j + 1) * LANES] = tile[low - first : high - first]
            if j == 0:
                spare = PART - 1 if c == 0 else 0
                row = tile[spare : spare + 1]
        for r in range(low, high):
            out_ref[r : r + 1, TILES * LANES :] = row[:, (r - first) * REST : (r - first + 1) * REST]


def exchange(value, axes):
    return lax.all_to_all(value, axes, split_axis=0, concat_axis=0, tiled=True)


def shift(value, axis, by):
    size = lax.axis_size(axis)
    return lax.ppermute(value, axis, [(i, (i + by) % size) for i in range(size)])


def call(kernel, out_shape, scratch, args, mib, space=pltpu.VMEM):
    spaces = [pltpu.SMEM if a.dtype == jnp.int32 else space for a in args]
    outs = jax.tree.map(
        lambda o: pl.BlockSpec(memory_space=pltpu.SMEM if o.dtype == jnp.int32 else pltpu.VMEM),
        out_shape,
    )
    return pl.pallas_call(
        kernel,
        out_shape=out_shape,
        in_specs=[pl.BlockSpec(memory_space=space) for space in spaces],
        out_specs=outs,
        scratch_shapes=scratch,
        compiler_params=pltpu.CompilerParams(vmem_limit_bytes=mib and mib * MIB),
        cost_estimate=pl.CostEstimate(flops=0, bytes_accessed=6 * MIB, transcendentals=0),
    )(*args)


def gradient(counts, pixels, cotangent):
    n_enc, n_dp, nz = lax.axis_size(ENC), lax.axis_size(DP), lax.axis_size(Z)
    nx, ny = lax.axis_size("x"), lax.axis_size("y")
    me = lax.axis_index(ENC).astype(jnp.int32)[None]
    at = [lax.axis_index(ENC), lax.axis_index("core"), lax.axis_index("x")]
    at = jnp.concatenate([jnp.stack(at).astype(jnp.int32), counts[0]])
    pix, cot = pixels[0].T, cotangent[0].T
    width, depth = cot.shape
    bf16 = lambda *shape: jax.ShapeDtypeStruct(shape, jnp.bfloat16)
    f32 = lambda *shape: jax.ShapeDtypeStruct(shape, jnp.float32)
    rows = 2 * ny * PART

    messages = call(
        pack_kernel,
        bf16(n_enc, PAIRS, 2, LANES),
        [
            pltpu.VMEM((pix.shape[1], TILES * LANES), jnp.bfloat16),
            pltpu.VMEM(pix.shape, jnp.bfloat16),
            pltpu.SemaphoreType.DMA((pix.shape[1] // 256,)),
        ],
        (me, counts, pix),
        None,
        pltpu.HBM,
    )
    arrived = exchange(messages, ENC)
    cuts = call(
        cut_kernel,
        [bf16(2, rows, depth)] * nx,
        [pltpu.VMEM((width, depth), jnp.float32), pltpu.VMEM((nx, 2, rows, depth), jnp.bfloat16)],
        (at, cot),
        12,
    )
    cuts = [cuts[0]] + [shift(cuts[d], "x", d) for d in range(1, nx)]
    source = call(trace_kernel, jax.ShapeDtypeStruct((depth // BLK,), jnp.int32), [], (at,), 1)
    placed = call(place_kernel, bf16(nx, depth + 2 * REST, TILES * LANES), [], (source, arrived), 8)
    placed, cuts = lax.optimization_barrier((placed, cuts))
    row = exchange(placed, "x")
    keep, send = call(
        grad_kernel,
        [f32(ny, 2 * HALF, LANES)] * 2,
        [pltpu.VMEM((2, rows, (TILES + 1) * LANES), jnp.float32)],
        (at, *cuts, row),
        16,
    )
    terms = keep + shift(send, "core", 1)
    terms = jnp.sum(exchange(terms.reshape(ny * nz, -1, LANES), ("y", *Z)), axis=0)
    parts = exchange(jnp.broadcast_to(terms, (n_dp, *terms.shape)), DP)
    return call(unpack_kernel, f32(width // n_enc, pix.shape[0]), [], (parts,), 8)


def solution(mesh):
    torus = Mesh(mesh.devices.reshape(6, 2, 2, 8, 4), ("zl", "core", "zh", "y", "x"))
    return jax.shard_map(
        gradient,
        mesh=torus,
        in_specs=(P(DP, None), P(DP, ENC, None), P(DP, ENC, None)),
        out_specs=P(ENC, None),
        check_vma=False,
    )
```

```python
import jax
import jax.numpy as jnp
from jax import lax
from jax.experimental import pallas as pl
from jax.experimental.pallas import tpu as pltpu
from jax.sharding import Mesh
from jax.sharding import PartitionSpec as P


BLK = 16
LANES = 128
TILES = 3
REST = 8
PAIRS = TILES * BLK // 2 + 1
PART = 16
HALF = TILES * PART
ENC = ("zh", "y", "x")
Z = ("zh", "zl")
DP = ("zl", "core")
FIRST = 3
MIB = 1024 * 1024


def pack_kernel(me_ref, counts_ref, pix_ref, out_ref, rows_ref):
    n_enc = out_ref.shape[0]
    whole, patches = rows_ref.shape[1], pix_ref.shape[1]
    side = 256
    me = me_ref[0]
    start = lax.fori_loop(
        0,
        n_enc,
        lambda e, total: total + jnp.where(e < me, counts_ref[0, e], 0),
        0,
        unroll=8,
    )
    eye = (
        lax.broadcasted_iota(jnp.int32, (side, side), 0)
        == lax.broadcasted_iota(jnp.int32, (side, side), 1)
    ).astype(jnp.bfloat16)
    column = lax.broadcasted_iota(jnp.int32, (REST, LANES), 0)
    mine = lax.broadcasted_iota(jnp.int32, (REST, LANES), 1) // BLK == column
    per_tile = LANES // BLK
    for b in range(patches // side):
        turned = lax.dot_general(
            eye,
            pix_ref[:whole, b * side : (b + 1) * side],
            (((1,), (1,)), ((), ())),
            preferred_element_type=jnp.float32,
        )
        rows_ref[b * side : (b + 1) * side, :] = turned.astype(jnp.bfloat16)
        rests = []
        for tile in range(b * side // LANES, (b + 1) * side // LANES):
            rest = pix_ref[whole:, tile * LANES : (tile + 1) * LANES].astype(jnp.float32)
            rests.append(pltpu.roll(rest, 0, 1, stride=BLK, stride_axis=0))
        for i in range(side // BLK):
            s = b * (side // BLK) + i
            t = lax.rem(start + s, n_enc)
            for j in range(TILES):
                block = rows_ref[s * BLK : (s + 1) * BLK, j * LANES : (j + 1) * LANES]
                out_ref[t, j * BLK // 2 : (j + 1) * BLK // 2] = block.reshape(BLK // 2, 2, LANES)
            rest = pltpu.roll(rests[i // per_tile], -i % per_tile * BLK, 1)
            row = jnp.sum(jnp.where(mine, rest, 0.0), axis=0, keepdims=True)
            out_ref[t, PAIRS - 1] = jnp.broadcast_to(row, (2, LANES)).astype(jnp.bfloat16)


def cut_kernel(at_ref, cot_ref, *refs):
    *out_refs, wide_ref, cut_ref = refs
    nx, _, rows, _ = cut_ref.shape
    shards = rows // PART
    own = cot_ref.shape[0] // (nx * shards)
    step = cot_ref.shape[0] // 4
    for m in range(4):
        at = slice(m * step, (m + 1) * step)
        wide_ref[at, :] = cot_ref[at, :].astype(jnp.float32)

    def cut(pair, _):
        base = pl.multiple_of(pair * (2 * nx * own), 8)
        for zh in range(2):
            for b in range(2 * nx):
                to = pl.multiple_of(pair * (4 * PART), PART) + (b // nx * 2 + zh) * PART
                for c in range(2):
                    first = zh * nx * (shards // 2) * own + b * own + c * (own - PART)
                    low = first // 8 * 8
                    span = pl.cdiv(first - low + PART, 8) * 8
                    part = wide_ref[pl.ds(pl.multiple_of(base + low, 8), span), :][
                        first - low : first - low + PART
                    ]
                    cut_ref[b % nx, c, pl.ds(pl.multiple_of(to, PART), PART), :] = part.astype(
                        jnp.bfloat16
                    )
        return 0

    lax.fori_loop(0, shards // 4, cut, 0)
    for d, out_ref in enumerate(out_refs):
        out_ref[...] = cut_ref[lax.rem(at_ref[2] + d, nx)]


def trace_kernel(at_ref, from_ref):
    n_enc = at_ref.shape[0] - FIRST

    def trace(e, start):
        count = at_ref[FIRST + e]
        slot = lax.rem(at_ref[0] - lax.rem(start, n_enc) + n_enc, n_enc)

        @pl.when(slot < count)
        def _():
            from_ref[(start + slot) // n_enc] = e

        return start + count

    lax.fori_loop(0, n_enc, trace, 0)


def place_kernel(from_ref, arrived_ref, out_ref):
    depth = out_ref.shape[2]
    column = lax.broadcasted_iota(jnp.int32, (REST, LANES), 0)
    lane = lax.broadcasted_iota(jnp.int32, (REST, LANES), 1)
    per_tile = LANES // BLK
    rests = []
    for k in range(depth // BLK):
        e = from_ref[k]
        for j in range(TILES):
            block = arrived_ref[e, j * BLK // 2 : (j + 1) * BLK // 2]
            out_ref[0, k * BLK : (k + 1) * BLK, j * LANES : (j + 1) * LANES] = block.reshape(
                BLK, LANES
            )
        row = arrived_ref[e, PAIRS - 1].astype(jnp.float32)[:1]
        here = k % per_tile
        moved = pltpu.roll(jnp.broadcast_to(row, (REST, LANES)), here * BLK, 1)
        for by in (1, 2, 4):
            back = pltpu.roll(moved, LANES - by * BLK, 1)
            moved = jnp.where(column // by % 2 == 1, back, moved)
        if here == 0:
            rests.append(moved)
        else:
            rests[-1] = jnp.where(lane // BLK == here, moved, rests[-1])
    rest = jnp.concatenate(rests, axis=1)
    out_ref[0, depth:, :] = jnp.concatenate([rest, rest], axis=0).astype(jnp.bfloat16)
    for i in range(1, out_ref.shape[0]):
        out_ref[i] = out_ref[0]


def grad_kernel(at_ref, *refs):
    keep_ref, send_ref, sums_ref = refs[-3:]
    *cut_refs, pix_ref = refs[:-3]
    nx = len(cut_refs)
    rows, depth = cut_refs[0].shape[1:]
    for c in range(2):
        whole = rest = 0.0
        for d, cut_ref in enumerate(cut_refs):
            came = lax.rem(at_ref[2] + nx - d, nx)
            cut = cut_ref[c]
            whole += jnp.dot(cut, pix_ref[came, :depth, :], preferred_element_type=jnp.float32)
            spread = jnp.concatenate([pix_ref[came, depth:, :]] * (LANES // (2 * REST)), axis=0)
            rest += lax.dot_general(
                cut, spread, (((1,), (1,)), ((), ())), preferred_element_type=jnp.float32
            )
        sums_ref[c, :, : TILES * LANES] = whole
        sums_ref[c, :, TILES * LANES :] = rest
    place = lax.broadcasted_iota(jnp.int32, (PART, LANES), 0)
    mine = lax.broadcasted_iota(jnp.int32, (PART, LANES), 1) // REST == place
    for out_ref, c in ((keep_ref, at_ref[1]), (send_ref, 1 - at_ref[1])):
        spare = jnp.where(c == 0, PART - 1, 0)
        for q in range(rows // PART):
            y, zh = q // 2, q % 2
            at = slice(q * PART, (q + 1) * PART)
            row = jnp.sum(
                jnp.where(mine, sums_ref[c, at, TILES * LANES :], 0.0), axis=0, keepdims=True
            )
            for j in range(TILES):
                tile = sums_ref[c, at, j * LANES : (j + 1) * LANES]
                if j == 0:
                    tile = jnp.where(place == spare, row, tile)
                out_ref[y, zh * HALF + j * PART : zh * HALF + (j + 1) * PART, :] = tile


def unpack_kernel(parts_ref, out_ref):
    own = out_ref.shape[0]
    cut = own // 2 + 1
    for c, low, high, first in ((0, 0, cut, 0), (1, cut, own, own - PART)):
        for j in range(TILES):
            tile = jnp.concatenate([parts_ref[4 * j + c], parts_ref[4 * j + 2 + c]], axis=0)
            out_ref[low:high, j * LANES : (j + 1) * LANES] = tile[low - first : high - first]
            if j == 0:
                spare = PART - 1 if c == 0 else 0
                row = tile[spare : spare + 1]
        for r in range(low, high):
            out_ref[r : r + 1, TILES * LANES :] = row[:, (r - first) * REST : (r - first + 1) * REST]


def exchange(value, axes):
    return lax.all_to_all(value, axes, split_axis=0, concat_axis=0, tiled=True)


def shift(value, axis, by):
    size = lax.axis_size(axis)
    return lax.ppermute(value, axis, [(i, (i + by) % size) for i in range(size)])


def call(kernel, out_shape, scratch, args, mib):
    spaces = [pltpu.SMEM if a.dtype == jnp.int32 else pltpu.VMEM for a in args]
    outs = jax.tree.map(
        lambda o: pl.BlockSpec(memory_space=pltpu.SMEM if o.dtype == jnp.int32 else pltpu.VMEM),
        out_shape,
    )
    return pl.pallas_call(
        kernel,
        out_shape=out_shape,
        in_specs=[pl.BlockSpec(memory_space=space) for space in spaces],
        out_specs=outs,
        scratch_shapes=scratch,
        compiler_params=pltpu.CompilerParams(vmem_limit_bytes=mib and mib * MIB),
        cost_estimate=pl.CostEstimate(flops=0, bytes_accessed=6 * MIB, transcendentals=0),
    )(*args)


def gradient(counts, pixels, cotangent):
    n_enc, n_dp, nz = lax.axis_size(ENC), lax.axis_size(DP), lax.axis_size(Z)
    nx, ny = lax.axis_size("x"), lax.axis_size("y")
    me = lax.axis_index(ENC).astype(jnp.int32)[None]
    at = [lax.axis_index(ENC), lax.axis_index("core"), lax.axis_index("x")]
    at = jnp.concatenate([jnp.stack(at).astype(jnp.int32), counts[0]])
    pix, cot = pixels[0].T, cotangent[0].T
    width, depth = cot.shape
    bf16 = lambda *shape: jax.ShapeDtypeStruct(shape, jnp.bfloat16)
    f32 = lambda *shape: jax.ShapeDtypeStruct(shape, jnp.float32)
    rows = 2 * ny * PART

    messages = call(
        pack_kernel,
        bf16(n_enc, PAIRS, 2, LANES),
        [pltpu.VMEM((pix.shape[1], TILES * LANES), jnp.bfloat16)],
        (me, counts, pix),
        None,
    )
    arrived = exchange(messages, ENC)
    cuts = call(
        cut_kernel,
        [bf16(2, rows, depth)] * nx,
        [pltpu.VMEM((width, depth), jnp.float32), pltpu.VMEM((nx, 2, rows, depth), jnp.bfloat16)],
        (at, cot),
        12,
    )
    cuts = [cuts[0]] + [shift(cuts[d], "x", d) for d in range(1, nx)]
    source = call(trace_kernel, jax.ShapeDtypeStruct((depth // BLK,), jnp.int32), [], (at,), 1)
    placed = call(place_kernel, bf16(nx, depth + 2 * REST, TILES * LANES), [], (source, arrived), 8)
    placed, cuts = lax.optimization_barrier((placed, cuts))
    row = exchange(placed, "x")
    keep, send = call(
        grad_kernel,
        [f32(ny, 2 * HALF, LANES)] * 2,
        [pltpu.VMEM((2, rows, (TILES + 1) * LANES), jnp.float32)],
        (at, *cuts, row),
        16,
    )
    terms = keep + shift(send, "core", 1)
    terms = jnp.sum(exchange(terms.reshape(ny * nz, -1, LANES), ("y", *Z)), axis=0)
    parts = exchange(jnp.broadcast_to(terms, (n_dp, *terms.shape)), DP)
    return call(unpack_kernel, f32(width // n_enc, pix.shape[0]), [], (parts,), 8)


def solution(mesh):
    torus = Mesh(mesh.devices.reshape(6, 2, 2, 8, 4), ("zl", "core", "zh", "y", "x"))
    return jax.shard_map(
        gradient,
        mesh=torus,
        in_specs=(P(DP, None), P(DP, ENC, None), P(DP, ENC, None)),
        out_specs=P(ENC, None),
        check_vma=False,
    )
```

```python
import jax
import jax.numpy as jnp
from jax import lax
from jax.experimental import pallas as pl
from jax.experimental.pallas import tpu as pltpu
from jax.sharding import Mesh
from jax.sharding import PartitionSpec as P


BLK = 16
LANES = 128
TILES = 3
REST = 8
PAIRS = TILES * BLK // 2 + 1
PART = 16
HALF = TILES * PART
ENC = ("zh", "y", "x")
Z = ("zh", "zl")
DP = ("zl", "core")
FIRST = 3
MIB = 1024 * 1024


def pack_kernel(me_ref, counts_ref, pix_ref, out_ref):
    n_enc = out_ref.shape[0]
    whole, patches = TILES * LANES, pix_ref.shape[1]
    side = 256
    me = me_ref[0]
    start = lax.fori_loop(
        0,
        n_enc,
        lambda e, total: total + jnp.where(e < me, counts_ref[0, e], 0),
        0,
        unroll=8,
    )
    eye = (
        lax.broadcasted_iota(jnp.int32, (side, side), 0)
        == lax.broadcasted_iota(jnp.int32, (side, side), 1)
    ).astype(jnp.bfloat16)
    column = lax.broadcasted_iota(jnp.int32, (REST, LANES), 0)
    mine = lax.broadcasted_iota(jnp.int32, (REST, LANES), 1) // BLK == column
    per_tile = LANES // BLK
    for b in range(patches // side):
        turned = lax.dot_general(
            eye,
            pix_ref[:whole, b * side : (b + 1) * side],
            (((1,), (1,)), ((), ())),
            preferred_element_type=jnp.float32,
        )
        turned = turned.astype(jnp.bfloat16)
        rests = []
        for tile in range(b * side // LANES, (b + 1) * side // LANES):
            rest = pix_ref[whole:, tile * LANES : (tile + 1) * LANES].astype(jnp.float32)
            rests.append(pltpu.roll(rest, 0, 1, stride=BLK, stride_axis=0))
        for i in range(side // BLK):
            s = b * (side // BLK) + i
            t = lax.rem(start + s, n_enc)
            for j in range(TILES):
                block = turned[i * BLK : (i + 1) * BLK, j * LANES : (j + 1) * LANES]
                out_ref[t, j * BLK // 2 : (j + 1) * BLK // 2] = block.reshape(BLK // 2, 2, LANES)
            rest = pltpu.roll(rests[i // per_tile], -i % per_tile * BLK, 1)
            row = jnp.sum(jnp.where(mine, rest, 0.0), axis=0, keepdims=True)
            out_ref[t, PAIRS - 1] = jnp.broadcast_to(row, (2, LANES)).astype(jnp.bfloat16)


def cut_kernel(at_ref, cot_ref, *refs):
    *out_refs, wide_ref, cut_ref = refs
    nx, _, rows, _ = cut_ref.shape
    shards = rows // PART
    own = cot_ref.shape[0] // (nx * shards)
    step = cot_ref.shape[0] // 4
    for m in range(4):
        at = slice(m * step, (m + 1) * step)
        wide_ref[at, :] = cot_ref[at, :].astype(jnp.float32)

    def cut(pair, _):
        base = pl.multiple_of(pair * (2 * nx * own), 8)
        for zh in range(2):
            for b in range(2 * nx):
                to = pl.multiple_of(pair * (4 * PART), PART) + (b // nx * 2 + zh) * PART
                for c in range(2):
                    first = zh * nx * (shards // 2) * own + b * own + c * (own - PART)
                    low = first // 8 * 8
                    span = pl.cdiv(first - low + PART, 8) * 8
                    part = wide_ref[pl.ds(pl.multiple_of(base + low, 8), span), :][
                        first - low : first - low + PART
                    ]
                    cut_ref[b % nx, c, pl.ds(pl.multiple_of(to, PART), PART), :] = part.astype(
                        jnp.bfloat16
                    )
        return 0

    lax.fori_loop(0, shards // 4, cut, 0)
    for d, out_ref in enumerate(out_refs):
        out_ref[...] = cut_ref[lax.rem(at_ref[2] + d, nx)]


def trace_kernel(at_ref, from_ref):
    n_enc = at_ref.shape[0] - FIRST

    def trace(e, start):
        count = at_ref[FIRST + e]
        slot = lax.rem(at_ref[0] - lax.rem(start, n_enc) + n_enc, n_enc)

        @pl.when(slot < count)
        def _():
            from_ref[(start + slot) // n_enc] = e

        return start + count

    lax.fori_loop(0, n_enc, trace, 0)


def place_kernel(from_ref, arrived_ref, out_ref):
    depth = out_ref.shape[2]
    column = lax.broadcasted_iota(jnp.int32, (REST, LANES), 0)
    lane = lax.broadcasted_iota(jnp.int32, (REST, LANES), 1)
    per_tile = LANES // BLK
    rests = []
    for k in range(depth // BLK):
        e = from_ref[k]
        for j in range(TILES):
            block = arrived_ref[e, j * BLK // 2 : (j + 1) * BLK // 2]
            out_ref[0, k * BLK : (k + 1) * BLK, j * LANES : (j + 1) * LANES] = block.reshape(
                BLK, LANES
            )
        row = arrived_ref[e, PAIRS - 1].astype(jnp.float32)[:1]
        here = k % per_tile
        moved = pltpu.roll(jnp.broadcast_to(row, (REST, LANES)), here * BLK, 1)
        for by in (1, 2, 4):
            back = pltpu.roll(moved, LANES - by * BLK, 1)
            moved = jnp.where(column // by % 2 == 1, back, moved)
        if here == 0:
            rests.append(moved)
        else:
            rests[-1] = jnp.where(lane // BLK == here, moved, rests[-1])
    rest = jnp.concatenate(rests, axis=1)
    out_ref[0, depth:, :] = jnp.concatenate([rest, rest], axis=0).astype(jnp.bfloat16)
    for i in range(1, out_ref.shape[0]):
        out_ref[i] = out_ref[0]


def grad_kernel(at_ref, *refs):
    keep_ref, send_ref, sums_ref = refs[-3:]
    *cut_refs, pix_ref = refs[:-3]
    nx = len(cut_refs)
    rows, depth = cut_refs[0].shape[1:]
    for c in range(2):
        whole = rest = 0.0
        for d, cut_ref in enumerate(cut_refs):
            came = lax.rem(at_ref[2] + nx - d, nx)
            cut = cut_ref[c]
            whole += jnp.dot(cut, pix_ref[came, :depth, :], preferred_element_type=jnp.float32)
            spread = jnp.concatenate([pix_ref[came, depth:, :]] * (LANES // (2 * REST)), axis=0)
            rest += lax.dot_general(
                cut, spread, (((1,), (1,)), ((), ())), preferred_element_type=jnp.float32
            )
        sums_ref[c, :, : TILES * LANES] = whole
        sums_ref[c, :, TILES * LANES :] = rest
    place = lax.broadcasted_iota(jnp.int32, (PART, LANES), 0)
    mine = lax.broadcasted_iota(jnp.int32, (PART, LANES), 1) // REST == place
    for out_ref, c in ((keep_ref, at_ref[1]), (send_ref, 1 - at_ref[1])):
        spare = jnp.where(c == 0, PART - 1, 0)
        for q in range(rows // PART):
            y, zh = q // 2, q % 2
            at = slice(q * PART, (q + 1) * PART)
            row = jnp.sum(
                jnp.where(mine, sums_ref[c, at, TILES * LANES :], 0.0), axis=0, keepdims=True
            )
            for j in range(TILES):
                tile = sums_ref[c, at, j * LANES : (j + 1) * LANES]
                if j == 0:
                    tile = jnp.where(place == spare, row, tile)
                out_ref[y, zh * HALF + j * PART : zh * HALF + (j + 1) * PART, :] = tile


def unpack_kernel(parts_ref, out_ref):
    own = out_ref.shape[0]
    cut = own // 2 + 1
    for c, low, high, first in ((0, 0, cut, 0), (1, cut, own, own - PART)):
        for j in range(TILES):
            tile = jnp.concatenate([parts_ref[4 * j + c], parts_ref[4 * j + 2 + c]], axis=0)
            out_ref[low:high, j * LANES : (j + 1) * LANES] = tile[low - first : high - first]
            if j == 0:
                spare = PART - 1 if c == 0 else 0
                row = tile[spare : spare + 1]
        for r in range(low, high):
            out_ref[r : r + 1, TILES * LANES :] = row[:, (r - first) * REST : (r - first + 1) * REST]


def exchange(value, axes):
    return lax.all_to_all(value, axes, split_axis=0, concat_axis=0, tiled=True)


def shift(value, axis, by):
    size = lax.axis_size(axis)
    return lax.ppermute(value, axis, [(i, (i + by) % size) for i in range(size)])


def call(kernel, out_shape, scratch, args, mib):
    spaces = [pltpu.SMEM if a.dtype == jnp.int32 else pltpu.VMEM for a in args]
    outs = jax.tree.map(
        lambda o: pl.BlockSpec(memory_space=pltpu.SMEM if o.dtype == jnp.int32 else pltpu.VMEM),
        out_shape,
    )
    return pl.pallas_call(
        kernel,
        out_shape=out_shape,
        in_specs=[pl.BlockSpec(memory_space=space) for space in spaces],
        out_specs=outs,
        scratch_shapes=scratch,
        compiler_params=pltpu.CompilerParams(vmem_limit_bytes=mib and mib * MIB),
        cost_estimate=pl.CostEstimate(flops=0, bytes_accessed=6 * MIB, transcendentals=0),
    )(*args)


def gradient(counts, pixels, cotangent):
    n_enc, n_dp, nz = lax.axis_size(ENC), lax.axis_size(DP), lax.axis_size(Z)
    nx, ny = lax.axis_size("x"), lax.axis_size("y")
    me = lax.axis_index(ENC).astype(jnp.int32)[None]
    at = [lax.axis_index(ENC), lax.axis_index("core"), lax.axis_index("x")]
    at = jnp.concatenate([jnp.stack(at).astype(jnp.int32), counts[0]])
    pix, cot = pixels[0].T, cotangent[0].T
    width, depth = cot.shape
    bf16 = lambda *shape: jax.ShapeDtypeStruct(shape, jnp.bfloat16)
    f32 = lambda *shape: jax.ShapeDtypeStruct(shape, jnp.float32)
    rows = 2 * ny * PART

    messages = call(
        pack_kernel,
        bf16(n_enc, PAIRS, 2, LANES),
        [],
        (me, counts, pix),
        None,
    )
    arrived = exchange(messages, ENC)
    cuts = call(
        cut_kernel,
        [bf16(2, rows, depth)] * nx,
        [pltpu.VMEM((width, depth), jnp.float32), pltpu.VMEM((nx, 2, rows, depth), jnp.bfloat16)],
        (at, cot),
        12,
    )
    cuts = [cuts[0]] + [shift(cuts[d], "x", d) for d in range(1, nx)]
    source = call(trace_kernel, jax.ShapeDtypeStruct((depth // BLK,), jnp.int32), [], (at,), 1)
    placed = call(place_kernel, bf16(nx, depth + 2 * REST, TILES * LANES), [], (source, arrived), 8)
    placed, cuts = lax.optimization_barrier((placed, cuts))
    row = exchange(placed, "x")
    keep, send = call(
        grad_kernel,
        [f32(ny, 2 * HALF, LANES)] * 2,
        [pltpu.VMEM((2, rows, (TILES + 1) * LANES), jnp.float32)],
        (at, *cuts, row),
        16,
    )
    terms = keep + shift(send, "core", 1)
    terms = jnp.sum(exchange(terms.reshape(ny * nz, -1, LANES), ("y", *Z)), axis=0)
    parts = exchange(jnp.broadcast_to(terms, (n_dp, *terms.shape)), DP)
    return call(unpack_kernel, f32(width // n_enc, pix.shape[0]), [], (parts,), 8)


def solution(mesh):
    torus = Mesh(mesh.devices.reshape(6, 2, 2, 8, 4), ("zl", "core", "zh", "y", "x"))
    return jax.shard_map(
        gradient,
        mesh=torus,
        in_specs=(P(DP, None), P(DP, ENC, None), P(DP, ENC, None)),
        out_specs=P(ENC, None),
        check_vma=False,
    )
```
